32 devices in a mesh: groups: 2 (over x), seq: 16 (over z, y, core).
Axes of the slice: x: 2, y: 2, z: 4, core: 2. Of those that a mesh axis runs over, the one named last changes fastest.
Arguments:
- clip_tokens: bfloat16 [32, 128, 512], P(('groups', 'seq')), parts along dimension 0, may hold values from -6 to 6
- spatial_qkv: bfloat16 [512, 1536], replicated, may hold values from -4.6403883 to 4.6403883
- spatial_out: bfloat16 [512, 512], replicated, may hold values from -0.5 to 0.5
- temporal_qkv: bfloat16 [512, 1536], replicated, may hold values from -4.6403883 to 4.6403883
- temporal_out: bfloat16 [512, 512], replicated, may hold values from -0.5 to 0.5
- mlp_up: bfloat16 [512, 2048], replicated, may hold values from -0.25 to 0.25
- mlp_down: bfloat16 [2048, 512], replicated, may hold values from -0.25 to 0.25
Outputs:
- layer_out: bfloat16 [32, 128, 512], P(('groups', 'seq')), parts along dimension 0
The draws below stay inside these ranges and needn't reach their ends.
There are 2 independent parts, one for each index of `groups`. The reference program is written for one: setup_inputs(seed, part) draws one part's arguments, and reference() takes and returns one part's arrays. A program takes and returns all parts, laid end to end along the dimension named above; an argument that names none is the same for every part. Nothing has to cross between parts.
All inputs are finite; a program needn't handle non-finite values.
Results may differ from the reference program's by a relative error of at most 0.013.
Values may be sent and summed in bfloat16 or wider, within the bound.
A program may use at most 128 MiB of HBM per device.

```python
import jax
import jax.numpy as jnp
from jax import lax

D = 512
HEADS = 8
HEAD_DIM = 64
FF = 2048
PATCH_DEV = 8
FRAMES = 16
PATCHES = 128


def projection_draw(key):
    scale = D ** (-0.5)
    matrix_draw = jnp.clip(jax.random.normal(key, (D, 3 * D), jnp.float32), -5.0, 5.0) * scale
    return matrix_draw.astype(jnp.bfloat16)


def draw_spatial_qkv(key, part):
    return projection_draw(jax.random.fold_in(key, 101))


def draw_temporal_qkv(key, part):
    return projection_draw(jax.random.fold_in(key, 202))


def shard_levels(rng, dims, shards, smallest, top_value):
    def one(axis_at, shards_of):
        steps = jax.random.uniform(jax.random.fold_in(jax.random.fold_in(rng, 6), axis_at), (shards_of,), jnp.float32, smallest / len(shards), top_value / len(shards))
        return jnp.repeat(jnp.exp(steps), dims[axis_at] // shards_of).reshape((-1,) + (1,) * (len(dims) - axis_at - 1))

    gain = one(*shards[0])
    for cut in shards[1:]:
        gain = gain * one(*cut)
    return gain


def gaussian(key, extent, deviation, reach, split=(), held_as=jnp.bfloat16):
    drawn = jax.random.normal(key, extent, jnp.float32) * deviation
    if len(split) > 0:
        drawn = shard_levels(key, extent, split, -0.22, 0.18) * drawn
    return jnp.clip(drawn, min=-reach, max=reach).astype(held_as)


def setup_inputs(seed: int = 0, part: int = 0) -> dict:
    streams_of = jax.random.split(jax.random.key(seed), 8)
    own_keys = jax.random.split(jax.random.fold_in(streams_of[7], part), 8)
    clip_tokens = gaussian(own_keys[0], (FRAMES, PATCHES, D), 1.0, 6.0, ((0, 16),))
    spatial_qkv = draw_spatial_qkv(jax.random.fold_in(streams_of[7], 71), part)
    spatial_out = gaussian(streams_of[2], (D, D), (D // 4) ** -0.5, 0.5)
    temporal_qkv = draw_temporal_qkv(jax.random.fold_in(streams_of[7], 71), part)
    temporal_out = gaussian(streams_of[4], (D, D), (D // 4) ** -0.5, 0.5)
    mlp_up = gaussian(streams_of[5], (D, FF), D ** -0.5, 0.25)
    mlp_down = gaussian(streams_of[6], (FF, D), (FF // 4) ** -0.5, 0.25)
    return {"clip_tokens": clip_tokens, "spatial_qkv": spatial_qkv, "spatial_out": spatial_out, "temporal_qkv": temporal_qkv, "temporal_out": temporal_out, "mlp_up": mlp_up, "mlp_down": mlp_down}


def norm_rows(values):
    center = values - lax.optimization_barrier(jnp.mean(values, axis=-1, keepdims=True))
    spread = lax.optimization_barrier(jnp.mean(center * center, axis=-1, keepdims=True))
    return (center * lax.rsqrt(spread + 1e-05)).astype(jnp.bfloat16)

def softmax_rows(scores):
    row_max = lax.optimization_barrier(jnp.max(scores, axis=-1, keepdims=True))
    raised = jnp.exp(scores - row_max)
    return (raised / lax.optimization_barrier(jnp.sum(raised, axis=-1, keepdims=True))).astype(jnp.bfloat16)

def spatial_frame(frame_rows, w_qkv, w_out):
    packed = jnp.dot(norm_rows(frame_rows.astype(jnp.float32)), w_qkv, preferred_element_type=jnp.float32)
    packed = packed.astype(jnp.bfloat16).reshape(PATCHES, 3, HEADS, HEAD_DIM).astype(jnp.float32)
    scores = jnp.einsum('qhd,khd->hqk', packed[:, 0], packed[:, 1]) * HEAD_DIM ** (-0.5)
    weights = softmax_rows(scores).astype(jnp.float32)
    attended = jnp.einsum('hqk,khd->qhd', weights, packed[:, 2]).astype(jnp.bfloat16).reshape(PATCHES, D)
    merged = frame_rows.astype(jnp.float32) + jnp.dot(attended, w_out, preferred_element_type=jnp.float32)
    return merged.astype(jnp.bfloat16)

def temporal_block(tokens, w_qkv, w_out):
    frames, count_rows, model_width = tokens.shape
    flat_rows = tokens.reshape(frames * count_rows, model_width)
    packed = jnp.dot(norm_rows(flat_rows.astype(jnp.float32)), w_qkv, preferred_element_type=jnp.float32)
    packed = packed.astype(jnp.bfloat16).reshape(frames, count_rows, 3, HEADS, HEAD_DIM).astype(jnp.float32)
    scores = jnp.einsum('fkhd,gkhd->khfg', packed[:, :, 0], packed[:, :, 1]) * HEAD_DIM ** (-0.5)
    weights = softmax_rows(scores).astype(jnp.float32)
    attended = jnp.einsum('khfg,gkhd->fkhd', weights, packed[:, :, 2]).astype(jnp.bfloat16)
    attended = attended.reshape(frames * count_rows, model_width)
    merged = flat_rows.astype(jnp.float32) + jnp.dot(attended, w_out, preferred_element_type=jnp.float32)
    return merged.astype(jnp.bfloat16)

def feed_forward(tokens, w_up, w_down):
    raised = jnp.dot(norm_rows(tokens.astype(jnp.float32)), w_up, preferred_element_type=jnp.float32)
    hidden = jax.nn.gelu(raised, approximate=True).astype(jnp.bfloat16)
    merged = tokens.astype(jnp.float32) + jnp.dot(hidden, w_down, preferred_element_type=jnp.float32)
    return merged.astype(jnp.bfloat16)

def reference(clip_tokens, spatial_qkv, spatial_out, temporal_qkv, temporal_out, mlp_up, mlp_down):
    mixed = lax.map(lambda frame_rows: spatial_frame(frame_rows, spatial_qkv, spatial_out), clip_tokens)
    blocks = mixed.reshape(FRAMES, PATCHES // PATCH_DEV, PATCH_DEV, D).transpose(1, 0, 2, 3)

    def one_block(tokens):
        after_time = temporal_block(tokens, temporal_qkv, temporal_out)
        return feed_forward(after_time, mlp_up, mlp_down).reshape(FRAMES, PATCH_DEV, D)
    finished = lax.map(one_block, blocks)
    return finished.transpose(1, 0, 2, 3).reshape(FRAMES, PATCHES, D)
```

```python
import functools
import math

import jax
import jax.numpy as jnp
from jax import lax
from jax.experimental import pallas as pl
from jax.experimental.pallas import tpu as pltpu
from jax.sharding import PartitionSpec as P

HEADS = 8
LANES = 128
VMEM_BYTES = 67043328
SHARES = (1, 1, 2, 0)
ORDERS = ((2, 1, 0, 3), (2, 0, 1, 3), (0, 1, 2, 3), (2, 0, 1, 3))
QUARTERS = len(SHARES)
MESH = pl.DeviceIdType.MESH
F32 = jnp.float32
BF16 = jnp.bfloat16
S = jax.named_scope


def norm_rows(values):
    center = values - jnp.mean(values, axis=-1, keepdims=True)
    spread = jnp.mean(center * center, axis=-1, keepdims=True)
    return (center * lax.rsqrt(spread + 1e-05)).astype(BF16)


def gelu(u):
    return 0.5 * u * (1.0 + jnp.tanh(math.sqrt(2.0 / math.pi) * (u + 0.044715 * (u * u * u))))


def dot(a, b):
    return jnp.dot(a, b, preferred_element_type=F32)


def blocks_of(count, body):
    if count <= 2:
        for i in range(count):
            body(i)
    else:
        def step(i, carry):
            body(i)
            return carry

        lax.fori_loop(0, count, step, 0)


def attend(packed, query_row, keys, rows, width, head_width, same_slot):
    per_block = LANES // head_width
    total = sum(count for _, count in keys)
    lane = lax.broadcasted_iota(jnp.int32, (total, LANES), 1)
    own = [(lane >= h * head_width) & (lane < (h + 1) * head_width) for h in range(per_block)]
    ones = jnp.concatenate([jnp.where(mask, 1.0, 0.0).astype(BF16) for mask in own], axis=0)
    scale = head_width ** (-0.5) * math.log2(math.e)
    if same_slot:
        query_at = lax.broadcasted_iota(jnp.int32, (rows, total), 0)
        key_at = lax.broadcasted_iota(jnp.int32, (rows, total), 1)
        allowed = lax.rem(query_at, same_slot) == lax.rem(key_at, same_slot)

    def spread(block, band):
        at = pl.ds(band * width + block * LANES, LANES)
        values = jnp.concatenate([packed[pl.ds(first, count), at] for first, count in keys], axis=0)
        return jnp.concatenate([jnp.where(mask, values, jnp.zeros_like(values)) for mask in own], axis=0)

    scores, weights, outs = [], [], []
    for block in range(width // LANES):
        q = packed[pl.ds(query_row, rows), pl.ds(block * LANES, LANES)]
        scores.append(lax.dot_general(q, spread(block, 1), (((1,), (1,)), ((), ())), preferred_element_type=F32))
    for both in scores:
        raised = []
        for h in range(per_block):
            one = both[:, h * total:(h + 1) * total]
            if same_slot:
                one = jnp.where(allowed, one, -1e30)
            top = jnp.max(one, axis=-1, keepdims=True)
            raised.append(jnp.exp2((one - top) * scale).astype(BF16))
        weights.append(jnp.concatenate(raised, axis=1))
    for block, weight in enumerate(weights):
        both = dot(weight, jnp.concatenate([spread(block, 2), ones], axis=1))
        outs.append((both[:, :LANES] / both[:, LANES:]).astype(BF16))
    return jnp.concatenate(outs, axis=1)


def kernel(
    n, x_hbm, wq1_hbm, wo1_hbm, wq2_hbm, wo2_hbm, up_hbm, down_hbm, out_v,
    x_v, wq1, wo1, wq2, wo2, up, down, packed, send1, recv1, send2,
    load_sem, send1_sem, recv1_sem, send2_sem, recv2_sem,
):
    _, slot, width = x_v.shape
    total = n * slot
    head_width = width // HEADS
    quarter = n // QUARTERS
    starts = [sum(SHARES[:i]) * quarter for i in range(QUARTERS)]
    me = lax.axis_index("seq")
    mine = me // quarter
    place = lax.rem(me, quarter)

    loads = [
        pltpu.make_async_copy(src, dst, load_sem.at[i]) for i, (src, dst) in enumerate(
            ((x_hbm, x_v), (wq1_hbm, wq1), (wo1_hbm, wo1), (wq2_hbm, wq2), (wo2_hbm, wo2), (up_hbm, up), (down_hbm, down))
        )
    ]
    wide = 2 * width
    pair_load = pltpu.make_async_copy(wq1_hbm.at[:, pl.ds(0, wide)], wq1.at[:, pl.ds(0, wide)], load_sem.at[1])
    value_load = pltpu.make_async_copy(wq1_hbm.at[:, pl.ds(wide, width)], wq1.at[:, pl.ds(wide, width)], load_sem.at[7])
    loads[0].start()
    pair_load.start()
    value_load.start()
    loads[2].start()

    def each_of(group, body):
        def visit(j):
            at = lax.rem(place + j, quarter)
            body(group * quarter + at, at)

        @pl.when(mine != group)
        def _():
            visit(0)

        if quarter <= 8:
            for j in range(1, quarter):
                visit(j)
        else:
            def step(j, carry):
                visit(j)
                return carry

            lax.fori_loop(1, quarter, step, 0)

    barrier = pltpu.get_barrier_semaphore()

    def greet(peer, at):
        pl.semaphore_signal(barrier, inc=1, device_id={"seq": peer}, device_id_type=MESH)

    owners = [g for g in range(QUARTERS) if SHARES[g]]

    def if_owner(body):
        if len(owners) == QUARTERS:
            body()
        else:
            pl.when(functools.reduce(jnp.logical_or, [mine == g for g in owners]))(body)

    def greet_all():
        for g in range(QUARTERS):
            each_of(g, greet)

    if_owner(greet_all)

    def copy1(peer, source, at, s):
        return pltpu.make_async_remote_copy(
            src_ref=send1.at[source], dst_ref=recv1.at[s * n + at], send_sem=send1_sem,
            recv_sem=recv1_sem, device_id={"seq": peer}, device_id_type=MESH,
        )

    def copy2(peer, source, at):
        return pltpu.make_async_remote_copy(
            src_ref=send2.at[source], dst_ref=out_v.at[at], send_sem=send2_sem,
            recv_sem=recv2_sem, device_id={"seq": peer}, device_id_type=MESH,
        )

    def wait_bytes(buffer, count, sem):
        some = buffer.at[pl.ds(0, count)]
        pltpu.make_async_copy(some, some, sem).wait()

    row_block = min(128, total)
    block_slots = row_block // slot

    def project(source, weights, i, rows):
        values = source[pl.ds(i * (rows // slot), rows // slot)].astype(F32).reshape(rows, width)
        packed[pl.ds(i * rows, rows), :] = dot(norm_rows(values), weights[...]).astype(BF16)

    with S("xwait"):
        loads[0].wait()
    for i in range(3, 7):
        loads[i].start()

    def spatial(i):
        at = pl.ds(i * block_slots, block_slots)
        heads = attend(packed, i * row_block, [(0, total)], row_block, width, head_width, 0)
        merged = x_v[at].astype(F32).reshape(row_block, width) + dot(heads, wo1[...])
        send1[at] = merged.reshape(block_slots, slot, width).astype(BF16)

    with S("proj1"):
        if total == row_block:
            normed = norm_rows(x_v[...].astype(F32).reshape(total, width))
            pair_load.wait()
            packed[pl.ds(0, total), pl.ds(0, wide)] = dot(normed, wq1[:, pl.ds(0, wide)]).astype(BF16)
            value_load.wait()
            loads[2].wait()
            packed[pl.ds(0, total), pl.ds(wide, width)] = dot(normed, wq1[:, pl.ds(wide, width)]).astype(BF16)
            spatial(0)
        else:
            pair_load.wait()
            value_load.wait()
            loads[2].wait()
            blocks_of(total // row_block, lambda i: project(x_v, wq1, i, row_block))
            blocks_of(total // row_block, spatial)
    with S("barrier"):
        pl.semaphore_wait(barrier, len(owners) * quarter - functools.reduce(lambda a, b: a + b, [(mine == g).astype(jnp.int32) for g in owners]))

    def send_first(groups):
        for g in groups:
            def give(peer, at, g=g):
                for s in range(SHARES[g]):
                    copy1(peer, starts[g] + at * SHARES[g] + s, me, s).start()

            if SHARES[g]:
                each_of(g, give)

    for g in range(QUARTERS):
        pl.when(mine == g)(functools.partial(send_first, ORDERS[g]))

    with S("loads"):
        for i in range(3, 7):
            loads[i].wait()

    def first_slot(share):
        same = [g for g in range(QUARTERS) if SHARES[g] == share]
        base = starts[same[0]]
        for g in same[1:]:
            base = jnp.where(mine == g, starts[g], base)
        return base + place * share

    def temporal(share):
        span = share * total
        base = first_slot(share)
        for s in range(share):
            recv1[s * n + me] = send1[base + s]
        with S("recv1"):
            wait_bytes(recv1, share * (n - 1), recv1_sem)
        rows = span if total <= 128 else row_block
        with S("proj2"):
            blocks_of(span // rows, lambda i: project(recv1, wq2, i, rows))
        part = row_block // share
        frames = part // slot

        def joined(pieces):
            return pieces[0] if share == 1 else jnp.concatenate(pieces, axis=0)

        def block(i):
            ranges = [pl.ds(s * n + i * frames, frames) for s in range(share)]
            heads = joined([
                attend(packed, s * total + i * part, [(s * total, total)], part, width, head_width, slot)
                for s in range(share)
            ])
            values = joined([recv1[at].astype(F32).reshape(part, width) for at in ranges])
            after = (values + dot(heads, wo2[...])).astype(BF16).astype(F32)
            hidden = gelu(dot(norm_rows(after), up[...])).astype(BF16)
            done = after + dot(hidden, down[...])
            for s, at in enumerate(ranges):
                send2[at] = done[s * part:(s + 1) * part].reshape(frames, slot, width).astype(BF16)

            def give(j):
                peer = i * frames + j

                @pl.when(peer != me)
                def _():
                    for s in range(share):
                        copy2(peer, s * n + peer, base + s).start()

            for j in range(frames):
                give(j)

        with S("temp"):
            blocks_of(total // part, block)

        for s in range(share):
            out_v[base + s] = send2[s * n + me]
        with S("wsend"):
            wait_bytes(send1, n - share, send1_sem)
            wait_bytes(send2, share * (n - 1), send2_sem)
        with S("recv2"):
            wait_bytes(out_v, n - share, recv2_sem)

    def watch():
        with S("wsend"):
            wait_bytes(send1, n, send1_sem)
        with S("recv2"):
            wait_bytes(out_v, n, recv2_sem)

    for share in sorted(set(SHARES)):
        body = functools.partial(temporal, share) if share else watch
        pl.when(functools.reduce(jnp.logical_or, [mine == g for g in range(QUARTERS) if SHARES[g] == share]))(body)


def solution(mesh):
    n = mesh.shape["seq"]

    def local(clip_tokens, *weights):
        frames, patches, width = clip_tokens.shape
        assert frames == 1 and n % QUARTERS == 0
        slot = patches // n
        blocks = (n, slot, width)
        most = max(SHARES)
        held = (most * n, slot, width)
        vmem = [pltpu.VMEM(w.shape, w.dtype) for w in weights]
        out = pl.pallas_call(
            functools.partial(kernel, n),
            out_shape=pltpu.VMEM(blocks, BF16),
            in_specs=[pl.BlockSpec(memory_space=pltpu.HBM)] * 7,
            out_specs=pl.BlockSpec(memory_space=pltpu.VMEM),
            scratch_shapes=[
                pltpu.VMEM(blocks, BF16),
                *vmem,
                pltpu.VMEM((most * patches, 3 * width), BF16),
                pltpu.VMEM(blocks, BF16),
                pltpu.VMEM(held, BF16),
                pltpu.VMEM(held, BF16),
                pltpu.SemaphoreType.DMA((8,)),
                pltpu.SemaphoreType.DMA,
                pltpu.SemaphoreType.DMA,
                pltpu.SemaphoreType.DMA,
                pltpu.SemaphoreType.DMA,
            ],
            compiler_params=pltpu.CompilerParams(collective_id=0, has_side_effects=True, vmem_limit_bytes=VMEM_BYTES - math.prod(blocks) * 2 - 65536),
            name="layer",
        )(clip_tokens.reshape(blocks), *weights)
        return out.reshape(frames, patches, width)

    in_specs = (P(("groups", "seq"), None, None), P(), P(), P(), P(), P(), P())
    out_specs = P(("groups", "seq"), None, None)
    return jax.shard_map(local, mesh=mesh, in_specs=in_specs, out_specs=out_specs, check_vma=False)
```
